128 devices in a mesh: tile: 16 (over y_lo, x, core), subap: 8 (over y_hi, z).
Axes of the slice: x: 4, y: 4 (y_hi: 2, y_lo: 2; y = y_hi * 2 + y_lo), z: 4, core: 2. Of those that a mesh axis runs over, the one named last changes fastest.
Arguments:
- pulses: bfloat16 [16, 8, 2, 128, 16384], P('tile', 'subap'), may hold values from -6 to 6
- footprint: int32 [16, 8, 32], P('tile', 'subap'), may hold values from 0 to 47, as said below
- offsets: int32 [48], replicated, may hold values from 0 to 15872
- azimuth: bfloat16 [48, 16, 8, 2, 256, 128], P('tile', None, 'subap'), may hold values from -0.09375 to 0.09375
- range_interp: bfloat16 [48, 2, 512, 256], P('tile'), may hold values from -0.1875 to 0.1875
Outputs:
- image: float32 [48, 2, 256, 256], P('tile', None, 'subap')
The draws below stay inside these ranges and needn't reach their ends.
Inputs may be any that keep to these rules, and one draw needn't show every extreme that they name: For every o, footprint[k, s, o * 2 : (o + 1) * 2] holds 2 different tiles of o * 3 to (o + 1) * 3 - 1.
All inputs are finite; a program needn't handle non-finite values.
Results may differ from the reference program's by a relative error of at most 0.0029.
Values may be sent and summed in bfloat16 or wider, within the bound.
No kernel may reach another device: no remote copies, remote signals or barrier semaphores. Data moves between devices by JAX's collectives and lax.ppermute only.
A program may use at most 128 MiB of HBM per device.

```python
import jax
import jax.numpy as jnp
from jax import lax

RANGE = 16384
PB = 128
RW = 512
TA = 256
TR = 256
TILE_DEV = 3
CAP = 2
TILES = 48
SRC = 16
SUBAPS = 8


def draw_footprint(key, part):
    owners = TILES // TILE_DEV
    popular = jax.random.randint(jax.random.fold_in(key, 7), (owners, TILE_DEV), 0, 4)
    noise = jax.random.randint(jax.random.fold_in(key, 11), (SRC, SUBAPS, owners, TILE_DEV), 0, 64)
    scores = (noise + 32 * popular[None, None]) * TILE_DEV + jnp.arange(TILE_DEV, dtype=jnp.int32)
    chosen = lax.top_k(scores, CAP)[1].astype(jnp.int32)
    tiles = chosen + (jnp.arange(owners, dtype=jnp.int32) * TILE_DEV)[None, None, :, None]
    return tiles.reshape(SRC, SUBAPS, owners * CAP).astype(jnp.int32)


def plant(values, stream_key, least, largest):
    extent = values.shape
    spot = [jax.random.randint(jax.random.fold_in(stream_key, axis), (), 0, extent[axis]) for axis in range(len(extent))]
    values = values.at[tuple(spot)].set(least)
    longest = extent.index(max(extent))
    spot[longest] = (spot[longest] + 1) % extent[longest]
    return values.at[tuple(spot)].set(largest)


def shard_levels(own_key, extent, cuts, low, largest):
    gain, own = 1.0, jax.random.fold_in(own_key, 6)
    for position, shards_of in cuts:
        steps = jnp.exp(jax.random.uniform(jax.random.fold_in(own, position), (shards_of,), jnp.float32, low / len(cuts), largest / len(cuts)))
        gain = gain * jnp.repeat(steps, extent[position] // shards_of).reshape([-1 if axis == position else 1 for axis in range(len(extent))])
    return gain


def bell_draw(own_key, dims, spread, most, cuts=(), kind=jnp.bfloat16):
    result = jax.random.normal(own_key, dims, jnp.float32) * spread
    if len(cuts) > 0:
        result = shard_levels(own_key, dims, cuts, -0.22, 0.18) * result
    return jnp.clip(result, min=-most, max=most).astype(kind)


def setup_inputs(seed: int = 0) -> dict:
    splits = jax.random.split(jax.random.key(seed), 6)
    return {
        "pulses": bell_draw(splits[0], (SRC, SUBAPS, 2, PB, RANGE), 1.0, 6.0, ((0, 16), (1, 8))),
        "footprint": draw_footprint(jax.random.fold_in(splits[5], 71), 0),
        "offsets": plant(jax.random.randint(splits[2], (TILES,), 0, RANGE - RW + 1), jax.random.fold_in(splits[2], 1), 0, RANGE - RW).astype(jnp.int32),
        "azimuth": bell_draw(splits[3], (TILES, SRC, SUBAPS, 2, TA, PB), (2 * SRC * PB) ** -0.5, 0.09375, ((0, 16), (2, 8))),
        "range_interp": bell_draw(splits[4], (TILES, 2, RW, TR), (2 * RW) ** -0.5, 0.1875, ((0, 16),)),
    }


def combine(prod):
    real = prod[..., 0, 0, :, :] - prod[..., 1, 1, :, :]
    imag = prod[..., 0, 1, :, :] + prod[..., 1, 0, :, :]
    return jnp.stack([real, imag], axis=-3)

def reference(pulses, footprint, offsets, azimuth, range_interp):

    def one_tile(items):
        index, start, tile_az, table = items
        zero = jnp.zeros((), jnp.int32)
        window = lax.dynamic_slice(pulses, (zero, zero, zero, zero, start.astype(jnp.int32)), (SRC, SUBAPS, 2, PB, RW))
        hit = jnp.any(footprint == index, axis=-1).astype(pulses.dtype)
        window = window * hit[:, :, None, None, None]
        prod = jnp.einsum('kscpr,dru->kscdpu', window.astype(jnp.float32), table.astype(jnp.float32))
        ranged = combine(prod).astype(jnp.bfloat16)
        sub = combine(jnp.einsum('kscap,ksdpu->scdau', tile_az.astype(jnp.float32), ranged.astype(jnp.float32)))
        raw = lax.optimization_barrier(jnp.sum(sub, axis=0))
        power = jnp.mean(raw * raw)
        return raw / jnp.sqrt(power + 1e-06)
    tile_ids = jnp.arange(TILES, dtype=jnp.int32)
    return lax.map(one_tile, (tile_ids, offsets, azimuth, range_interp))
```

```python
import functools

import jax
import jax.numpy as jnp
from jax import lax
from jax.experimental import pallas as pl
from jax.experimental.pallas import tpu as pltpu
from jax.sharding import PartitionSpec as P

LANES = 128
ANY = pl.BlockSpec(memory_space=pl.ANY)
SMEM = pl.BlockSpec(memory_space=pltpu.SMEM)
VMEM = pl.BlockSpec(memory_space=pltpu.VMEM)


def extract_kernel(count, width, base_ref, shift_ref, block, out, wide, cut, in_sem, out_sem):
    span = wide.shape[2]

    def fetch(i):
        at = pl.multiple_of(base_ref[i], LANES)
        return pltpu.make_async_copy(block.at[:, pl.ds(at, span)], wide.at[i], in_sem.at[i])

    def send(i):
        return pltpu.make_async_copy(cut.at[i], out.at[i], out_sem.at[i])

    def first(i, c):
        fetch(i).start()
        return c

    lax.fori_loop(0, count, first, 0)

    def step(i, c):
        fetch(i).wait()
        rows = wide[i].astype(jnp.float32)
        turned = pltpu.roll(rows, span - shift_ref[i], 1)
        cut[i] = turned[:, :width].astype(cut.dtype)
        send(i).start()
        return c

    lax.fori_loop(0, count, step, 0)

    def last(i, c):
        send(i).wait()
        return c

    lax.fori_loop(0, count, last, 0)


def extract(block, base, shift, width):
    count, rows = base.shape[0], block.shape[0]
    span = width + LANES
    return pl.pallas_call(
        functools.partial(extract_kernel, count, width),
        out_shape=jax.ShapeDtypeStruct((count, rows, width), block.dtype),
        in_specs=[SMEM, SMEM, ANY],
        out_specs=ANY,
        scratch_shapes=[
            pltpu.VMEM((count, rows, span), block.dtype),
            pltpu.VMEM((count, rows, width), block.dtype),
            pltpu.SemaphoreType.DMA((count,)),
            pltpu.SemaphoreType.DMA((count,)),
        ],
        compiler_params=pltpu.CompilerParams(vmem_limit_bytes=48 << 20),
        cost_estimate=pl.CostEstimate(
            flops=0, transcendentals=0, bytes_accessed=count * rows * (span + width) * 2
        ),
    )(base, shift, block)


def compute_kernel(slots, local_ref, window, azimuth, table, out, sub, held, sem):
    source = pl.program_id(0)
    pulses = window.shape[2] // 2
    copies = []
    for slot in range(slots):
        tile = local_ref[source, slot]
        copies.append(
            pltpu.make_async_copy(azimuth.at[tile, source], held.at[slot], sem.at[slot])
        )
        copies[-1].start()

    @pl.when(source == 0)
    def _():
        sub[...] = jnp.zeros_like(sub)

    for slot in range(slots):
        tile = local_ref[source, slot]
        x = window[0, slot]
        pr = jnp.dot(x, table[tile, 0], preferred_element_type=jnp.float32)
        pi = jnp.dot(x, table[tile, 1], preferred_element_type=jnp.float32)
        rr = (pr[:pulses] - pi[pulses:]).astype(x.dtype)
        ri = (pi[:pulses] + pr[pulses:]).astype(x.dtype)
        right = jnp.concatenate(
            [jnp.concatenate([rr, ri], 1), jnp.concatenate([-ri, rr], 1)], 0
        )
        copies[slot].wait()
        left = jnp.concatenate([held[slot, 0], held[slot, 1]], 1)
        both = jnp.dot(left, right, preferred_element_type=jnp.float32)
        width = rr.shape[1]
        sub[tile, 0] += both[:, :width]
        sub[tile, 1] += both[:, width:]

    @pl.when(source == pl.num_programs(0) - 1)
    def _():
        groups, rows = out.shape[0], out.shape[3]
        for g in range(groups):
            out[g] = sub[:, :, g * rows : (g + 1) * rows, :].astype(out.dtype)


def compute(windows, local, azimuth, table, groups):
    sources, slots, both, width = windows.shape
    tiles, _, parts, height, pulses = azimuth.shape
    across = table.shape[3]
    rows = height // groups
    gs = pltpu.PrefetchScalarGridSpec(
        num_scalar_prefetch=1,
        grid=(sources,),
        in_specs=[
            pl.BlockSpec((1, slots, both, width), lambda i, l: (i, 0, 0, 0)),
            ANY,
            pl.BlockSpec(table.shape, lambda i, l: (0, 0, 0, 0)),
        ],
        out_specs=pl.BlockSpec((groups, tiles, parts, rows, across), lambda i, l: (0,) * 5),
        scratch_shapes=[
            pltpu.VMEM((tiles, parts, height, across), jnp.float32),
            pltpu.VMEM((slots, parts, height, pulses), azimuth.dtype),
            pltpu.SemaphoreType.DMA((slots,)),
        ],
    )
    return pl.pallas_call(
        functools.partial(compute_kernel, slots),
        out_shape=jax.ShapeDtypeStruct((groups, tiles, parts, rows, across), jnp.bfloat16),
        grid_spec=gs,
        compiler_params=pltpu.CompilerParams(vmem_limit_bytes=32 << 20),
    )(local, windows, azimuth, table)


def on_device(pulses, footprint, offsets, azimuth, range_interp):
    width = range_interp.shape[2]
    held = range_interp.shape[0]
    owners = lax.axis_size("tile")
    subaps = lax.axis_size("subap")
    block = pulses.reshape(-1, pulses.shape[-1])
    listed = footprint.reshape(owners, -1)
    slots = listed.shape[1]
    listed = jnp.sort(listed, axis=1)
    starts = jnp.take(offsets, listed.reshape(-1))
    base = jnp.minimum(starts // LANES * LANES, block.shape[1] - width - LANES)
    windows = extract(block, base, starts - base, width)
    windows = windows.reshape(owners, slots, block.shape[0], width)
    arrived = lax.all_to_all(windows, "tile", split_axis=0, concat_axis=0, tiled=True)
    local = lax.all_to_all(listed, "tile", split_axis=0, concat_axis=0, tiled=True)
    local = local - lax.axis_index("tile") * held
    parts = compute(arrived, local, azimuth[:, :, 0], range_interp, subaps)
    got = lax.all_to_all(parts, "subap", split_axis=0, concat_axis=0, tiled=True)
    raw = jnp.sum(got.astype(jnp.float32), axis=0)
    total = jnp.sum(raw * raw, axis=(1, 2, 3))
    hop = 1
    while hop < subaps:
        total = total + lax.ppermute(total, "subap", [(i, i ^ hop) for i in range(subaps)])
        hop *= 2
    power = total / (raw.size // held * subaps)
    return raw / jnp.sqrt(power + 1e-06)[:, None, None, None]


def solution(mesh):
    in_specs = (
        P("tile", "subap", None, None, None),
        P("tile", "subap", None),
        P(),
        P("tile", None, "subap", None, None, None),
        P("tile", None, None, None),
    )
    out_specs = P("tile", None, "subap", None)
    return jax.shard_map(
        on_device, mesh=mesh, in_specs=in_specs, out_specs=out_specs, check_vma=False
    )
```

```python
import functools

import jax
import jax.numpy as jnp
from jax import lax
from jax.experimental import pallas as pl
from jax.experimental.pallas import tpu as pltpu
from jax.sharding import PartitionSpec as P

LANES = 128
XS, CORES = 4, 2
ANY = pl.BlockSpec(memory_space=pl.ANY)
SMEM = pl.BlockSpec(memory_space=pltpu.SMEM)
VMEM = pl.BlockSpec(memory_space=pltpu.VMEM)


def place(index):
    return index // (XS * CORES), index // CORES % XS, index % CORES


def toward(index, dy, dx, dc):
    y, x, c = place(index)
    return ((y ^ dy) * XS + (x + dx) % XS) * CORES + (c ^ dc)


def pairs(count, dy, dx, dc):
    return [(i, toward(i, dy, dx, dc)) for i in range(count)]


def cut_kernel(pieces, held, footprint_hbm, offsets_hbm, block, *refs):
    outs, refs = refs[: len(pieces)], refs[len(pieces) :]
    footprint, offsets, wide, cut, note, scalar_sem, in_sem, out_sem, note_sem = refs
    scalars = [
        pltpu.make_async_copy(footprint_hbm, footprint, scalar_sem.at[0]),
        pltpu.make_async_copy(offsets_hbm, offsets, scalar_sem.at[1]),
    ]
    for copy in scalars:
        copy.start()
    me = lax.axis_index("tile")
    rows, span = wide.shape[1:]
    width = cut.shape[2]
    slots = outs[0].shape[1] // rows
    lane = lax.broadcasted_iota(jnp.int32, note.shape[1:], 1)
    for copy in scalars:
        copy.wait()
    steps, notes = [], []
    for out, (dy, dx, cores) in zip(outs, pieces):
        for at, dc in enumerate(cores):
            owner = toward(me, dy, dx, dc)
            ids = jnp.zeros(lane.shape, jnp.int32)
            for slot in range(slots):
                tile = footprint[owner * slots + slot]
                start = offsets[tile]
                base = jnp.minimum(start // LANES * LANES, block.shape[1] - span)
                i = len(steps)
                src = block.at[:, pl.ds(pl.multiple_of(base, LANES), span)]
                get = pltpu.make_async_copy(src, wide.at[i], in_sem.at[i])
                dst = out.at[at, slot * rows : (slot + 1) * rows]
                put = pltpu.make_async_copy(cut.at[i], dst, out_sem.at[i])
                get.start()
                steps.append((get, put, start - base))
                ids = jnp.where(lane // LANES == slot, tile - owner * held, ids)
            j = len(notes)
            note[j] = ids.astype(note.dtype)
            told = pltpu.make_async_copy(note.at[j], out.at[at, slots * rows :], note_sem.at[j])
            told.start()
            notes.append(told)
    for i, (get, put, shift) in enumerate(steps):
        get.wait()
        turned = pltpu.roll(wide[i].astype(jnp.float32), lax.rem(span - shift, span), 1)
        cut[i] = turned[:, :width].astype(cut.dtype)
        put.start()
    for _, put, _ in steps:
        put.wait()
    for told in notes:
        told.wait()


def cut_windows(pieces, footprint, offsets, block, held, slots, width):
    rows = block.shape[0]
    span = width + LANES
    whole = sum(len(cores) for _, _, cores in pieces)
    count = slots * whole
    return pl.pallas_call(
        functools.partial(cut_kernel, pieces, held),
        out_shape=[
            jax.ShapeDtypeStruct((len(cores), slots * rows + NOTE, width), block.dtype)
            for _, _, cores in pieces
        ],
        in_specs=[ANY] * 3,
        out_specs=[ANY] * len(pieces),
        scratch_shapes=[
            pltpu.SMEM(footprint.shape, footprint.dtype),
            pltpu.SMEM(offsets.shape, offsets.dtype),
            pltpu.VMEM((count, rows, span), block.dtype),
            pltpu.VMEM((count, rows, width), block.dtype),
            pltpu.VMEM((whole, NOTE, width), block.dtype),
            pltpu.SemaphoreType.DMA((2,)),
            pltpu.SemaphoreType.DMA((count,)),
            pltpu.SemaphoreType.DMA((count,)),
            pltpu.SemaphoreType.DMA((whole,)),
        ],
        compiler_params=pltpu.CompilerParams(vmem_limit_bytes=16 << 20),
        cost_estimate=pl.CostEstimate(
            flops=0, transcendentals=0, bytes_accessed=count * rows * (span + width) * 2
        ),
    )(footprint, offsets, block)


def add_kernel(sources, slots, first, last, *refs):
    windows, refs = refs[: len(sources)], refs[len(sources) :]
    azimuth, table, refs = refs[0], refs[1], refs[2:]
    if first:
        out, sub = refs
        sub[...] = jnp.zeros_like(sub)
    elif last:
        before, out, sub = refs
        sub[...] = before[...]
    else:
        before, out = refs
        sub = out
        sub[...] = before[...]
    me = lax.axis_index("tile")
    both = (windows[0].shape[1] - NOTE) // slots
    half = both // 2
    tiles = []
    for window in windows:
        note = window[0, slots * both :, :].astype(jnp.float32)
        for slot in range(slots):
            tile = jnp.max(note[:, slot * LANES : (slot + 1) * LANES])
            tiles.append(tile.astype(jnp.int32))
    for at, (window, (dy, dx, dc)) in enumerate(zip(windows, sources)):
        source = toward(me, dy, XS - dx, dc)
        for slot in range(slots):
            tile = tiles[at * slots + slot]
            x = window[0, slot * both : (slot + 1) * both]
            pr = jnp.dot(x, table[tile, 0], preferred_element_type=jnp.float32)
            pi = jnp.dot(x, table[tile, 1], preferred_element_type=jnp.float32)
            rr = (pr[:half] - pi[half:]).astype(x.dtype)
            ri = (pi[:half] + pr[half:]).astype(x.dtype)
            a = azimuth[tile, source]
            left = jnp.concatenate([a[0], a[1]], 1)
            sub[tile, 0] += jnp.dot(
                left, jnp.concatenate([rr, -ri], 0), preferred_element_type=jnp.float32
            )
            sub[tile, 1] += jnp.dot(
                left, jnp.concatenate([ri, rr], 0), preferred_element_type=jnp.float32
            )
    if last:
        rows = out.shape[3]
        for g in range(out.shape[0]):
            out[g] = sub[:, :, g * rows : (g + 1) * rows, :].astype(out.dtype)
    elif first:
        out[...] = sub[...]


def add(sources, slots, windows, azimuth, table, before, groups):
    tiles, _, parts, height, _ = azimuth.shape
    across = table.shape[3]
    whole = (tiles, parts, height, across)
    first, last = before is None, groups is not None
    shape = (groups, tiles, parts, height // groups, across) if last else whole
    operands = (*windows, azimuth, table) + (() if first else (before,))
    extra = first or last
    return pl.pallas_call(
        functools.partial(add_kernel, sources, slots, first, last),
        out_shape=jax.ShapeDtypeStruct(shape, jnp.bfloat16 if last else jnp.float32),
        in_specs=[VMEM] * len(operands),
        out_specs=VMEM,
        scratch_shapes=[pltpu.VMEM(whole, jnp.float32)] if extra else [],
        input_output_aliases={} if extra else {len(operands) - 1: 0},
        compiler_params=pltpu.CompilerParams(vmem_limit_bytes=16 << 20),
        cost_estimate=pl.CostEstimate(
            flops=len(sources) * 400_000_000, transcendentals=0, bytes_accessed=6_000_000
        ),
    )(*operands)


NOTE = 8
FLOWS = ((1, 2), (1, 1), (0, 3), (1, 3), (0, 1), (0, 2), (1, 0))
ROUNDS = ((0,), (1, 2), (3, 4), (5, 6))
AHEAD = 4


def after(x, y):
    return lax.optimization_barrier((x, y))


def on_device(pulses, footprint, offsets, azimuth, range_interp):
    held, _, width, _ = range_interp.shape
    owners = lax.axis_size("tile")
    subaps = lax.axis_size("subap")
    block = pulses.reshape(-1, pulses.shape[-1])
    footprint = footprint.reshape(-1)
    slots = footprint.shape[0] // owners
    azimuth = azimuth[:, :, 0]
    send = lambda x, dy, dx, dc: lax.ppermute(x, "tile", pairs(owners, dy, dx, dc))
    windows = []
    for at, flows in enumerate(ROUNDS):
        pieces = [(*FLOWS[f], (0, 1)) for f in flows]
        if at == 1:
            pieces += [(0, 0, (0,)), (0, 0, (1,))]
        made = cut_windows(pieces, footprint, offsets, block, held, slots, width)
        windows += made[: len(flows)]
        if at == 1:
            mine, other = made[len(flows) :]
            other = send(other, 0, 0, 1)
    got = []
    for f, w in enumerate(windows):
        if f >= AHEAD:
            w, got[f - AHEAD] = after(w, got[f - AHEAD])
        got.append(send(w, *FLOWS[f], 0))
    sub, ready, sources = None, [mine, other], [(0, 0, 0), (0, 0, 1)]
    for f, w in enumerate(got):
        dy, dx = FLOWS[f]
        passed = send(w[1:], 0, 0, 1)
        ready[0], w = after(ready[0], w)
        sub = add(sources, slots, ready, azimuth, range_interp, sub, None)
        if f + 1 < len(got):
            got[f + 1], sub = after(got[f + 1], sub)
        ready, sources = [w[:1], passed], [(dy, dx, 0), (dy, dx, 1)]
    sub = add(sources, slots, ready, azimuth, range_interp, sub, subaps)
    got = lax.all_to_all(sub, "subap", split_axis=0, concat_axis=0, tiled=True)
    raw = jnp.sum(got.astype(jnp.float32), axis=0)
    total = jnp.sum(raw * raw, axis=(1, 2, 3))
    hop = 1
    while hop < subaps:
        total = total + lax.ppermute(total, "subap", [(i, i ^ hop) for i in range(subaps)])
        hop *= 2
    power = total / (raw[0].size * subaps)
    return raw / jnp.sqrt(power + 1e-06)[:, None, None, None]


def solution(mesh):
    in_specs = (
        P("tile", "subap", None, None, None),
        P("tile", "subap", None),
        P(),
        P("tile", None, "subap", None, None, None),
        P("tile", None, None, None),
    )
    out_specs = P("tile", None, "subap", None)
    return jax.shard_map(
        on_device, mesh=mesh, in_specs=in_specs, out_specs=out_specs, check_vma=False
    )
```

```python
import functools

import jax
import jax.numpy as jnp
from jax import lax
from jax.experimental import pallas as pl
from jax.experimental.pallas import tpu as pltpu
from jax.sharding import PartitionSpec as P

LANES = 128
XS, CORES = 4, 2
ANY = pl.BlockSpec(memory_space=pl.ANY)
HBM = pl.BlockSpec(memory_space=pltpu.HBM)
VMEM = pl.BlockSpec(memory_space=pltpu.VMEM)


def place(index):
    return index // (XS * CORES), index // CORES % XS, index % CORES


def toward(index, dy, dx, dc):
    y, x, c = place(index)
    return ((y ^ dy) * XS + (x + dx) % XS) * CORES + (c ^ dc)


def pairs(count, dy, dx, dc):
    return [(i, toward(i, dy, dx, dc)) for i in range(count)]


def cut_kernel(pieces, fills, held, footprint_hbm, offsets_hbm, block, *refs):
    swapped, refs = (refs[0], refs[1:]) if fills else (None, refs)
    outs, refs = refs[: len(pieces)], refs[len(pieces) :]
    footprint, offsets, wide, cut, note, scalar_sem, in_sem, out_sem, note_sem, fill_sem = refs
    scalars = [
        pltpu.make_async_copy(footprint_hbm, footprint, scalar_sem.at[0]),
        pltpu.make_async_copy(offsets_hbm, offsets, scalar_sem.at[1]),
    ]
    for copy in scalars:
        copy.start()
    filling = []
    for n, (source, piece, at) in enumerate(fills):
        filling.append(
            pltpu.make_async_copy(swapped.at[source], outs[piece].at[at], fill_sem.at[n])
        )
        filling[-1].start()
    me = lax.axis_index("tile")
    rows, span = wide.shape[1:]
    width = cut.shape[2]
    slots = outs[0].shape[1] // rows
    lane = lax.broadcasted_iota(jnp.int32, note.shape[1:], 1)
    for copy in scalars:
        copy.wait()
    steps, notes = [], []
    for out, parts in zip(outs, pieces):
        for at, to in parts:
            owner = toward(me, *to)
            ids = jnp.zeros(lane.shape, jnp.int32)
            for slot in range(slots):
                tile = footprint[owner * slots + slot]
                start = offsets[tile]
                base = jnp.minimum(start // LANES * LANES, block.shape[1] - span)
                i = len(steps)
                src = block.at[:, pl.ds(pl.multiple_of(base, LANES), span)]
                get = pltpu.make_async_copy(src, wide.at[i], in_sem.at[i])
                dst = out.at[at, slot * rows : (slot + 1) * rows]
                put = pltpu.make_async_copy(cut.at[i], dst, out_sem.at[i])
                get.start()
                steps.append((get, put, start - base))
                ids = jnp.where(lane // LANES == slot, tile - owner * held, ids)
            j = len(notes)
            note[j] = ids.astype(note.dtype)
            told = pltpu.make_async_copy(note.at[j], out.at[at, slots * rows :], note_sem.at[j])
            told.start()
            notes.append(told)
    for i, (get, put, shift) in enumerate(steps):
        get.wait()
        turned = pltpu.roll(wide[i].astype(jnp.float32), lax.rem(span - shift, span), 1)
        cut[i] = turned[:, :width].astype(cut.dtype)
        put.start()
    for _, put, _ in steps:
        put.wait()
    for copy in notes + filling:
        copy.wait()


def cut_windows(pieces, sizes, fills, footprint, offsets, block, held, slots, width, swapped=None):
    rows = block.shape[0]
    span = width + LANES
    whole = sum(len(parts) for parts in pieces)
    count = slots * whole
    operands = (footprint, offsets, block) + (() if swapped is None else (swapped,))
    return pl.pallas_call(
        functools.partial(cut_kernel, pieces, fills, held),
        out_shape=[
            jax.ShapeDtypeStruct((size, slots * rows + NOTE, width), block.dtype)
            for size in sizes
        ],
        in_specs=[HBM] * len(operands),
        out_specs=[ANY] * len(pieces),
        scratch_shapes=[
            pltpu.SMEM(footprint.shape, footprint.dtype),
            pltpu.SMEM(offsets.shape, offsets.dtype),
            pltpu.VMEM((count, rows, span), block.dtype),
            pltpu.VMEM((count, rows, width), block.dtype),
            pltpu.VMEM((whole, NOTE, width), block.dtype),
            pltpu.SemaphoreType.DMA((2,)),
            pltpu.SemaphoreType.DMA((count,)),
            pltpu.SemaphoreType.DMA((count,)),
            pltpu.SemaphoreType.DMA((whole,)),
            pltpu.SemaphoreType.DMA((max(len(fills), 1),)),
        ],
        compiler_params=pltpu.CompilerParams(vmem_limit_bytes=16 << 20),
        cost_estimate=pl.CostEstimate(
            flops=0, transcendentals=0, bytes_accessed=count * rows * (span + width) * 2
        ),
    )(*operands)


def add_kernel(sources, slots, first, last, *refs):
    count = len(sources)
    windows, refs = refs[:count], refs[count:]
    azimuth, table, refs = refs[0], refs[1], refs[2:]
    if first:
        (sub,) = refs
        sub[...] = jnp.zeros_like(sub)
    else:
        before, refs = refs[0], refs[1:]
        outs, sub = (refs[:-1], refs[-1]) if last else ((), refs[0])
        sub[...] = before[...]
    me = lax.axis_index("tile")
    both = (windows[0].shape[1] - NOTE) // slots
    half = both // 2
    work, packed = [], None
    for window, parts in zip(windows, sources):
        for at, (dy, dx, dc) in enumerate(parts):
            note = window[at, slots * both :, :].astype(jnp.float32)
            for slot in range(slots):
                ids = note[:, slot * LANES : (slot + 1) * LANES] * float(BASE ** len(work))
                packed = ids if packed is None else packed + ids
                x = (window, at, slice(slot * both, (slot + 1) * both))
                work.append((x, toward(me, dy, XS - dx, dc)))
    packed = jnp.max(packed).astype(jnp.int32)
    for n, ((window, at, span), source) in enumerate(work):
        tile = (packed >> (n * (BASE.bit_length() - 1))) & (BASE - 1)
        x = window[at, span]
        pr = jnp.dot(x, table[tile, 0], preferred_element_type=jnp.float32)
        pi = jnp.dot(x, table[tile, 1], preferred_element_type=jnp.float32)
        rr = (pr[:half] - pi[half:]).astype(x.dtype)
        ri = (pi[:half] + pr[half:]).astype(x.dtype)
        right = jnp.concatenate([rr, ri], 1)
        width = rr.shape[1]
        ar = jnp.dot(azimuth[tile, source, 0], right, preferred_element_type=jnp.float32)
        ai = jnp.dot(azimuth[tile, source, 1], right, preferred_element_type=jnp.float32)
        sub[tile, 0] += ar[:, :width] - ai[:, width:]
        sub[tile, 1] += ar[:, width:] + ai[:, :width]
    if last:
        z = lax.axis_index("subap") % ZS
        halves = sub.shape[2] // outs[0].shape[2] // ZS * 2
        rows = outs[0].shape[2] // halves
        for dz, out in enumerate(outs):
            for y in range(halves):
                at = pl.multiple_of(((z + dz) % ZS + y * ZS) * rows, rows)
                out[:, :, y * rows : (y + 1) * rows] = sub[:, :, pl.ds(at, rows)].astype(out.dtype)


def add(sources, slots, windows, azimuth, table, before, last):
    tiles, _, parts, height, _ = azimuth.shape
    whole = (tiles, parts, height, table.shape[3])
    first = before is None
    shape = jax.ShapeDtypeStruct(whole, jnp.float32)
    if last:
        cut = (tiles, parts, height // ZS, table.shape[3])
        shape = [
            jax.ShapeDtypeStruct(cut, jnp.bfloat16 if dz else jnp.float32) for dz in range(ZS)
        ]
    operands = (*windows, azimuth, table) + (() if first else (before,))
    return pl.pallas_call(
        functools.partial(add_kernel, sources, slots, first, last),
        out_shape=shape,
        in_specs=[VMEM] * len(operands),
        out_specs=[VMEM] * ZS if last else VMEM,
        scratch_shapes=[pltpu.VMEM(whole, jnp.float32)] if last else [],
        input_output_aliases={} if first or last else {len(operands) - 1: 0},
        compiler_params=pltpu.CompilerParams(vmem_limit_bytes=16 << 20),
        cost_estimate=pl.CostEstimate(
            flops=sum(len(p) for p in sources) * 400_000_000,
            transcendentals=0,
            bytes_accessed=6_000_000,
        ),
    )(*operands)


NOTE = 8
BASE = 4
ZS = 4
DIRECT = (1, 2)
FLOWS = ((1, 1), (0, 3), (0, 2), (1, 0), (1, 3), (0, 1))
EARLY = 3
AHEAD = 3


def after(x, y):
    return lax.optimization_barrier((x, y))


def on_device(pulses, footprint, offsets, azimuth, range_interp):
    held, _, width, _ = range_interp.shape
    owners = lax.axis_size("tile")
    pin = lambda x: pltpu.with_memory_space_constraint(x, pltpu.HBM)
    block = pin(pulses.reshape(-1, pulses.shape[-1]))
    footprint = pin(footprint.reshape(-1))
    slots = footprint.shape[0] // owners
    azimuth = azimuth[:, :, 0]
    send = lambda x, dy, dx, dc: lax.ppermute(x, "tile", pairs(owners, dy, dx, dc))
    cut = functools.partial(
        cut_windows,
        footprint=footprint,
        offsets=pin(offsets),
        block=block,
        held=held,
        slots=slots,
        width=width,
    )
    (first,) = cut([[(0, (*DIRECT, 0)), (1, (*DIRECT, 1))]], [2], [])
    first, cut.keywords["footprint"] = after(first, footprint)
    flows, made = [DIRECT], [first]
    for at, group in enumerate((FLOWS[:EARLY], FLOWS[EARLY:])):
        to = [(*f, 1) for f in group] + ([(0, 0, 1)] if at == 0 else [])
        (other,) = cut([list(enumerate(to))], [len(to)], [])
        other = send(other, 0, 0, 1)
        other, cut.keywords["footprint"] = after(other, cut.keywords["footprint"])
        to = [(*f, 0) for f in group] + ([(0, 0, 0)] if at == 0 else [])
        filled = cut(
            [[(0, t)] for t in to],
            [2] * len(to),
            [(n, n, 1) for n in range(len(to))],
            swapped=other,
        )
        flows += group
        made += filled[: len(group)]
        if at == 0:
            here = filled[-1]
    work = [([here], [[(0, 0, 0), (0, 0, 1)]])]
    sub, done = None, 0
    for f, (flow, w) in enumerate(zip(flows, made)):
        while done <= f - AHEAD:
            sub = add(work[done][1], slots, work[done][0], azimuth, range_interp, sub, False)
            done += 1
            w, sub = after(w, sub)
        w = send(w, *flow, 0)
        if f == 0:
            work.append(([w[:1], send(w[1:], 0, 0, 1)], [[(*flow, 0)], [(*flow, 1)]]))
        else:
            work.append(([w], [[(*flow, 0), (*flow, 1)]]))
    for windows, chips in work[done:-1]:
        sub = add(chips, slots, windows, azimuth, range_interp, sub, False)
    own, *away = add(work[-1][1], slots, work[-1][0], azimuth, range_interp, sub, True)

    subaps = lax.axis_size("subap")
    near = lambda x, dy, dz: lax.ppermute(
        x,
        "subap",
        [(i, (i // ZS ^ dy) * ZS + (i + dz) % ZS) for i in range(subaps)],
    )
    order = sorted(range(1, ZS), key=lambda dz: -min(dz, ZS - dz))
    for part in [near(away[dz - 1], 0, dz) for dz in order]:
        own = own + part.astype(jnp.float32)
    raw = own + near(own.astype(jnp.bfloat16), 1, 0).astype(jnp.float32)
    total = jnp.sum(raw * raw, axis=(1, 2, 3))
    total = total + sum(near(total, 0, dz) for dz in order)
    power = total / (raw[0].size * ZS)
    rows = raw.shape[2] // 2
    raw = lax.dynamic_slice_in_dim(raw, lax.axis_index("subap") // ZS * rows, rows, 2)
    return raw / jnp.sqrt(power + 1e-06)[:, None, None, None]


def solution(mesh):
    in_specs = (
        P("tile", "subap", None, None, None),
        P("tile", "subap", None),
        P(),
        P("tile", None, "subap", None, None, None),
        P("tile", None, None, None),
    )
    out_specs = P("tile", None, "subap", None)
    return jax.shard_map(
        on_device, mesh=mesh, in_specs=in_specs, out_specs=out_specs, check_vma=False
    )
```

```python
import functools

import jax
import jax.numpy as jnp
from jax import lax
from jax.experimental import pallas as pl
from jax.experimental.pallas import tpu as pltpu
from jax.sharding import PartitionSpec as P

LANES = 128
XS, CORES = 4, 2
ANY = pl.BlockSpec(memory_space=pl.ANY)
HBM = pl.BlockSpec(memory_space=pltpu.HBM)
VMEM = pl.BlockSpec(memory_space=pltpu.VMEM)


def place(index):
    return index // (XS * CORES), index // CORES % XS, index % CORES


def toward(index, dy, dx, dc):
    y, x, c = place(index)
    return ((y ^ dy) * XS + (x + dx) % XS) * CORES + (c ^ dc)


def pairs(count, dy, dx, dc):
    return [(i, toward(i, dy, dx, dc)) for i in range(count)]


def cut_kernel(pieces, fills, held, footprint_hbm, offsets_hbm, block, *refs):
    swapped, refs = (refs[0], refs[1:]) if fills else (None, refs)
    outs, refs = refs[: len(pieces)], refs[len(pieces) :]
    footprint, offsets, wide, cut, note, scalar_sem, in_sem, out_sem, note_sem, fill_sem = refs
    scalars = [
        pltpu.make_async_copy(footprint_hbm, footprint, scalar_sem.at[0]),
        pltpu.make_async_copy(offsets_hbm, offsets, scalar_sem.at[1]),
    ]
    for copy in scalars:
        copy.start()
    filling = []
    for n, (source, piece, at) in enumerate(fills):
        filling.append(
            pltpu.make_async_copy(swapped.at[source], outs[piece].at[at], fill_sem.at[n])
        )
        filling[-1].start()
    me = lax.axis_index("tile")
    rows, span = wide.shape[1:]
    width = cut.shape[2]
    slots = outs[0].shape[1] // rows
    lane = lax.broadcasted_iota(jnp.int32, note.shape[1:], 1)
    for copy in scalars:
        copy.wait()
    steps, notes = [], []
    for out, parts in zip(outs, pieces):
        for at, to in parts:
            owner = toward(me, *to)
            ids = jnp.zeros(lane.shape, jnp.int32)
            for slot in range(slots):
                tile = footprint[owner * slots + slot]
                start = offsets[tile]
                base = jnp.minimum(start // LANES * LANES, block.shape[1] - span)
                i = len(steps)
                src = block.at[:, pl.ds(pl.multiple_of(base, LANES), span)]
                get = pltpu.make_async_copy(src, wide.at[i], in_sem.at[i])
                dst = out.at[at, slot * rows : (slot + 1) * rows]
                put = pltpu.make_async_copy(cut.at[i], dst, out_sem.at[i])
                get.start()
                steps.append((get, put, start - base))
                ids = jnp.where(lane // LANES == slot, tile - owner * held, ids)
            j = len(notes)
            note[j] = ids.astype(note.dtype)
            told = pltpu.make_async_copy(note.at[j], out.at[at, slots * rows :], note_sem.at[j])
            told.start()
            notes.append(told)
    for i, (get, put, shift) in enumerate(steps):
        get.wait()
        turn = lax.rem(LANES - shift, LANES)
        inside = lax.broadcasted_iota(jnp.int32, (rows, LANES), 1) < LANES - shift
        turned = [
            pltpu.roll(wide[i, :, n * LANES : (n + 1) * LANES].astype(jnp.float32), turn, 1)
            for n in range(span // LANES)
        ]
        for n in range(width // LANES):
            cut[i, :, n * LANES : (n + 1) * LANES] = jnp.where(
                inside, turned[n], turned[n + 1]
            ).astype(cut.dtype)
        put.start()
    for _, put, _ in steps:
        put.wait()
    for copy in notes + filling:
        copy.wait()


def cut_windows(pieces, sizes, fills, footprint, offsets, block, held, slots, width, swapped=None):
    rows = block.shape[0]
    span = width + LANES
    whole = sum(len(parts) for parts in pieces)
    count = slots * whole
    operands = (footprint, offsets, block) + (() if swapped is None else (swapped,))
    return pl.pallas_call(
        functools.partial(cut_kernel, pieces, fills, held),
        out_shape=[
            jax.ShapeDtypeStruct((size, slots * rows + NOTE, width), block.dtype)
            for size in sizes
        ],
        in_specs=[HBM] * len(operands),
        out_specs=[ANY] * len(pieces),
        scratch_shapes=[
            pltpu.SMEM(footprint.shape, footprint.dtype),
            pltpu.SMEM(offsets.shape, offsets.dtype),
            pltpu.VMEM((count, rows, span), block.dtype),
            pltpu.VMEM((count, rows, width), block.dtype),
            pltpu.VMEM((whole, NOTE, width), block.dtype),
            pltpu.SemaphoreType.DMA((2,)),
            pltpu.SemaphoreType.DMA((count,)),
            pltpu.SemaphoreType.DMA((count,)),
            pltpu.SemaphoreType.DMA((whole,)),
            pltpu.SemaphoreType.DMA((max(len(fills), 1),)),
        ],
        compiler_params=pltpu.CompilerParams(vmem_limit_bytes=16 << 20),
        cost_estimate=pl.CostEstimate(
            flops=0, transcendentals=0, bytes_accessed=1000
        ),
    )(*operands)


def add_kernel(sources, slots, first, last, *refs):
    count = len(sources)
    windows, refs = refs[:count], refs[count:]
    azimuth, table, refs = refs[0], refs[1], refs[2:]
    if first:
        (sub,) = refs
        sub[...] = jnp.zeros_like(sub)
    else:
        before, refs = refs[0], refs[1:]
        outs, sub = (refs[:-1], refs[-1]) if last else ((), refs[0])
        sub[...] = before[...]
    me = lax.axis_index("tile")
    both = (windows[0].shape[1] - NOTE) // slots
    half = both // 2
    work, packed = [], None
    for window, parts in zip(windows, sources):
        for at, (dy, dx, dc) in enumerate(parts):
            note = window[at, slots * both :, :].astype(jnp.float32)
            for slot in range(slots):
                ids = note[:, slot * LANES : (slot + 1) * LANES] * float(BASE ** len(work))
                packed = ids if packed is None else packed + ids
                x = (window, at, slice(slot * both, (slot + 1) * both))
                work.append((x, toward(me, dy, XS - dx, dc)))
    packed = jnp.max(packed).astype(jnp.int32)
    for n, ((window, at, span), source) in enumerate(work):
        tile = (packed >> (n * (BASE.bit_length() - 1))) & (BASE - 1)
        x = window[at, span]
        pr = jnp.dot(x, table[tile, 0], preferred_element_type=jnp.float32)
        pi = jnp.dot(x, table[tile, 1], preferred_element_type=jnp.float32)
        rr = (pr[:half] - pi[half:]).astype(x.dtype)
        ri = (pi[:half] + pr[half:]).astype(x.dtype)
        right = jnp.concatenate([rr, ri], 1)
        width = rr.shape[1]
        ar = jnp.dot(azimuth[tile, source, 0], right, preferred_element_type=jnp.float32)
        ai = jnp.dot(azimuth[tile, source, 1], right, preferred_element_type=jnp.float32)
        sub[tile, 0] += ar[:, :width] - ai[:, width:]
        sub[tile, 1] += ar[:, width:] + ai[:, :width]
    if last:
        z = lax.axis_index("subap") % ZS
        halves = sub.shape[2] // outs[0].shape[2] // ZS * 2
        rows = outs[0].shape[2] // halves
        for dz, out in enumerate(outs):
            for y in range(halves):
                at = pl.multiple_of(((z + dz) % ZS + y * ZS) * rows, rows)
                out[:, :, y * rows : (y + 1) * rows] = sub[:, :, pl.ds(at, rows)].astype(out.dtype)


def add(sources, slots, windows, azimuth, table, before, last):
    tiles, _, parts, height, _ = azimuth.shape
    whole = (tiles, parts, height, table.shape[3])
    first = before is None
    shape = jax.ShapeDtypeStruct(whole, jnp.float32)
    if last:
        cut = (tiles, parts, height // ZS, table.shape[3])
        shape = [
            jax.ShapeDtypeStruct(cut, jnp.bfloat16 if dz else jnp.float32) for dz in range(ZS)
        ]
    operands = (*windows, azimuth, table) + (() if first else (before,))
    return pl.pallas_call(
        functools.partial(add_kernel, sources, slots, first, last),
        out_shape=shape,
        in_specs=[VMEM] * len(operands),
        out_specs=[VMEM] * ZS if last else VMEM,
        scratch_shapes=[pltpu.VMEM(whole, jnp.float32)] if last else [],
        input_output_aliases={} if first or last else {len(operands) - 1: 0},
        compiler_params=pltpu.CompilerParams(vmem_limit_bytes=16 << 20),
        cost_estimate=pl.CostEstimate(
            flops=sum(len(p) for p in sources) * 400_000_000,
            transcendentals=0,
            bytes_accessed=6_000_000,
        ),
    )(*operands)


NOTE = 8
BASE = 4
ZS = 4
DIRECT = (1, 2)
FLOWS = ((1, 1), (0, 3), (1, 3), (0, 1), (0, 2), (1, 0))
EARLY = 3
AHEAD = 3


def after(x, y):
    return lax.optimization_barrier((x, y))


def on_device(pulses, footprint, offsets, azimuth, range_interp):
    held, _, width, _ = range_interp.shape
    owners = lax.axis_size("tile")
    pin = lambda x: pltpu.with_memory_space_constraint(x, pltpu.HBM)
    block = pin(pulses.reshape(-1, pulses.shape[-1]))
    footprint = pin(footprint.reshape(-1))
    slots = footprint.shape[0] // owners
    azimuth = azimuth[:, :, 0]
    send = lambda x, dy, dx, dc: lax.ppermute(x, "tile", pairs(owners, dy, dx, dc))
    cut = functools.partial(
        cut_windows,
        footprint=footprint,
        offsets=pin(offsets),
        block=block,
        held=held,
        slots=slots,
        width=width,
    )
    lead = [(0, (*DIRECT, 0)), (1, (*DIRECT, 1))]
    flows, made = [DIRECT], []
    for at, group in enumerate((FLOWS[:EARLY], FLOWS[EARLY:])):
        to = [(*f, 1) for f in group] + ([(0, 0, 1)] if at == 0 else [])
        extra = [lead] if at == 0 else []
        *first, other = cut([*extra, list(enumerate(to))], [2] * len(extra) + [len(to)], [])
        made += first
        other = send(other, 0, 0, 1)
        other, cut.keywords["footprint"] = after(other, cut.keywords["footprint"])
        to = [(*f, 0) for f in group] + ([(0, 0, 0)] if at == 0 else [])
        filled = cut(
            [[(0, t)] for t in to],
            [2] * len(to),
            [(n, n, 1) for n in range(len(to))],
            swapped=other,
        )
        flows += group
        made += filled[: len(group)]
        if at == 0:
            here = filled[-1]
    work = [([here], [[(0, 0, 0), (0, 0, 1)]])]
    sub, done = None, 0
    for f, (flow, w) in enumerate(zip(flows, made)):
        while done <= f - AHEAD:
            sub = add(work[done][1], slots, work[done][0], azimuth, range_interp, sub, False)
            done += 1
            w, sub = after(w, sub)
        w = send(w, *flow, 0)
        if f == 0:
            work.append(([w[:1], send(w[1:], 0, 0, 1)], [[(*flow, 0)], [(*flow, 1)]]))
        else:
            work.append(([w], [[(*flow, 0), (*flow, 1)]]))
    for windows, chips in work[done:-1]:
        sub = add(chips, slots, windows, azimuth, range_interp, sub, False)
    own, *away = add(work[-1][1], slots, work[-1][0], azimuth, range_interp, sub, True)

    subaps = lax.axis_size("subap")
    near = lambda x, dy, dz: lax.ppermute(
        x,
        "subap",
        [(i, (i // ZS ^ dy) * ZS + (i + dz) % ZS) for i in range(subaps)],
    )
    order = sorted(range(1, ZS), key=lambda dz: -min(dz, ZS - dz))
    for part in [near(away[dz - 1], 0, dz) for dz in order]:
        own = own + part.astype(jnp.float32)
    raw = own + near(own.astype(jnp.bfloat16), 1, 0).astype(jnp.float32)
    total = jnp.sum(raw * raw, axis=(1, 2, 3))
    total = total + sum(near(total, 0, dz) for dz in order)
    power = total / (raw[0].size * ZS)
    rows = raw.shape[2] // 2
    raw = lax.dynamic_slice_in_dim(raw, lax.axis_index("subap") // ZS * rows, rows, 2)
    return raw / jnp.sqrt(power + 1e-06)[:, None, None, None]


def solution(mesh):
    in_specs = (
        P("tile", "subap", None, None, None),
        P("tile", "subap", None),
        P(),
        P("tile", None, "subap", None, None, None),
        P("tile", None, None, None),
    )
    out_specs = P("tile", None, "subap", None)
    return jax.shard_map(
        on_device, mesh=mesh, in_specs=in_specs, out_specs=out_specs, check_vma=False
    )
```

```python
import functools

import jax
import jax.numpy as jnp
from jax import lax
from jax.experimental import pallas as pl
from jax.experimental.pallas import tpu as pltpu
from jax.sharding import PartitionSpec as P

LANES = 128
XS, CORES = 4, 2
ANY = pl.BlockSpec(memory_space=pl.ANY)
HBM = pl.BlockSpec(memory_space=pltpu.HBM)
VMEM = pl.BlockSpec(memory_space=pltpu.VMEM)


def place(index):
    return index // (XS * CORES), index // CORES % XS, index % CORES


def toward(index, dy, dx, dc):
    y, x, c = place(index)
    return ((y ^ dy) * XS + (x + dx) % XS) * CORES + (c ^ dc)


def pairs(count, dy, dx, dc):
    return [(i, toward(i, dy, dx, dc)) for i in range(count)]


def cut_kernel(pieces, fills, held, footprint_hbm, offsets_hbm, block, *refs):
    swapped, refs = (refs[0], refs[1:]) if fills else (None, refs)
    outs, refs = refs[: len(pieces)], refs[len(pieces) :]
    footprint, offsets, wide, cut, note, scalar_sem, in_sem, out_sem, note_sem, fill_sem = refs
    scalars = [
        pltpu.make_async_copy(footprint_hbm, footprint, scalar_sem.at[0]),
        pltpu.make_async_copy(offsets_hbm, offsets, scalar_sem.at[1]),
    ]
    for copy in scalars:
        copy.start()
    filling = []
    for n, (source, piece, at) in enumerate(fills):
        filling.append(
            pltpu.make_async_copy(swapped.at[source], outs[piece].at[at], fill_sem.at[n])
        )
        filling[-1].start()
    me = lax.axis_index("tile")
    rows, span = wide.shape[1:]
    width = cut.shape[2]
    slots = outs[0].shape[1] // rows
    lane = lax.broadcasted_iota(jnp.int32, note.shape[1:], 1)
    for copy in scalars:
        copy.wait()
    steps, notes = [], []
    for out, parts in zip(outs, pieces):
        for at, to in parts:
            owner = toward(me, *to)
            ids = jnp.zeros(lane.shape, jnp.int32)
            for slot in range(slots):
                tile = footprint[owner * slots + slot]
                start = offsets[tile]
                base = jnp.minimum(start // LANES * LANES, block.shape[1] - span)
                i = len(steps)
                src = block.at[:, pl.ds(pl.multiple_of(base, LANES), span)]
                get = pltpu.make_async_copy(src, wide.at[i], in_sem.at[i])
                dst = out.at[at, slot * rows : (slot + 1) * rows]
                put = pltpu.make_async_copy(cut.at[i], dst, out_sem.at[i])
                get.start()
                steps.append((get, put, start - base))
                ids = jnp.where(lane // LANES == slot, tile - owner * held, ids)
            j = len(notes)
            note[j] = ids.astype(note.dtype)
            told = pltpu.make_async_copy(note.at[j], out.at[at, slots * rows :], note_sem.at[j])
            told.start()
            notes.append(told)
    for i, (get, put, shift) in enumerate(steps):
        get.wait()
        turn = lax.rem(LANES - shift, LANES)
        inside = lax.broadcasted_iota(jnp.int32, (rows, LANES), 1) < LANES - shift
        turned = [
            pltpu.roll(wide[i, :, n * LANES : (n + 1) * LANES].astype(jnp.float32), turn, 1)
            for n in range(span // LANES)
        ]
        for n in range(width // LANES):
            cut[i, :, n * LANES : (n + 1) * LANES] = jnp.where(
                inside, turned[n], turned[n + 1]
            ).astype(cut.dtype)
        put.start()
    for _, put, _ in steps:
        put.wait()
    for copy in notes + filling:
        copy.wait()


def cut_windows(pieces, sizes, fills, footprint, offsets, block, held, slots, width, swapped=None):
    rows = block.shape[0]
    span = width + LANES
    whole = sum(len(parts) for parts in pieces)
    count = slots * whole
    operands = (footprint, offsets, block) + (() if swapped is None else (swapped,))
    return pl.pallas_call(
        functools.partial(cut_kernel, pieces, fills, held),
        out_shape=[
            jax.ShapeDtypeStruct((size, slots * rows + NOTE, width), block.dtype)
            for size in sizes
        ],
        in_specs=[HBM] * len(operands),
        out_specs=[ANY] * len(pieces),
        scratch_shapes=[
            pltpu.SMEM(footprint.shape, footprint.dtype),
            pltpu.SMEM(offsets.shape, offsets.dtype),
            pltpu.VMEM((count, rows, span), block.dtype),
            pltpu.VMEM((count, rows, width), block.dtype),
            pltpu.VMEM((whole, NOTE, width), block.dtype),
            pltpu.SemaphoreType.DMA((2,)),
            pltpu.SemaphoreType.DMA((count,)),
            pltpu.SemaphoreType.DMA((count,)),
            pltpu.SemaphoreType.DMA((whole,)),
            pltpu.SemaphoreType.DMA((max(len(fills), 1),)),
        ],
        compiler_params=pltpu.CompilerParams(vmem_limit_bytes=16 << 20),
        cost_estimate=pl.CostEstimate(
            flops=0, transcendentals=0, bytes_accessed=1000
        ),
    )(*operands)


def add_kernel(sources, slots, first, last, *refs):
    count = len(sources)
    windows, refs = refs[:count], refs[count:]
    azimuth, table, refs = refs[0], refs[1], refs[2:]
    if first:
        (sub,) = refs
        sub[...] = jnp.zeros_like(sub)
    else:
        before, refs = refs[0], refs[1:]
        outs, sub = (refs[:-1], refs[-1]) if last else ((), refs[0])
        sub[...] = before[...]
    me = lax.axis_index("tile")
    both = (windows[0].shape[1] - NOTE) // slots
    half = both // 2
    work, packed = [], None
    for window, parts in zip(windows, sources):
        for at, (dy, dx, dc) in enumerate(parts):
            note = window[at, slots * both :, :].astype(jnp.float32)
            for slot in range(slots):
                ids = note[:, slot * LANES : (slot + 1) * LANES] * float(BASE ** len(work))
                packed = ids if packed is None else packed + ids
                x = (window, at, slice(slot * both, (slot + 1) * both))
                work.append((x, toward(me, dy, XS - dx, dc)))
    packed = jnp.max(packed).astype(jnp.int32)
    def in_range(n):
        (window, at, span), source = work[n]
        tile = (packed >> (n * (BASE.bit_length() - 1))) & (BASE - 1)
        x = window[at, span]
        pr = jnp.dot(x, table[tile, 0], preferred_element_type=jnp.float32)
        pi = jnp.dot(x, table[tile, 1], preferred_element_type=jnp.float32)
        rr = (pr[:half] - pi[half:]).astype(x.dtype)
        ri = (pi[:half] + pr[half:]).astype(x.dtype)
        return tile, source, rr, ri

    def in_azimuth(tile, source, rr, ri):
        left = jnp.concatenate([azimuth[tile, source, 0], azimuth[tile, source, 1]], 1)
        right = jnp.concatenate(
            [jnp.concatenate([rr, ri], 1), jnp.concatenate([-ri, rr], 1)], 0
        )
        both = jnp.dot(left, right, preferred_element_type=jnp.float32)
        sub[tile, 0] += both[:, : rr.shape[1]]
        sub[tile, 1] += both[:, rr.shape[1] :]

    for ranged in [in_range(n) for n in range(len(work))]:
        in_azimuth(*ranged)
    if last:
        z = lax.axis_index("subap") % ZS
        halves = sub.shape[2] // outs[0].shape[2] // ZS * 2
        rows = outs[0].shape[2] // halves
        for dz, out in enumerate(outs):
            for y in range(halves):
                at = pl.multiple_of(((z + dz) % ZS + y * ZS) * rows, rows)
                out[:, :, y * rows : (y + 1) * rows] = sub[:, :, pl.ds(at, rows)].astype(out.dtype)


def add(sources, slots, windows, azimuth, table, before, last):
    tiles, _, parts, height, _ = azimuth.shape
    whole = (tiles, parts, height, table.shape[3])
    first = before is None
    shape = jax.ShapeDtypeStruct(whole, jnp.float32)
    if last:
        cut = (tiles, parts, height // ZS, table.shape[3])
        shape = [
            jax.ShapeDtypeStruct(cut, jnp.bfloat16 if dz else jnp.float32) for dz in range(ZS)
        ]
    operands = (*windows, azimuth, table) + (() if first else (before,))
    return pl.pallas_call(
        functools.partial(add_kernel, sources, slots, first, last),
        out_shape=shape,
        in_specs=[VMEM] * len(operands),
        out_specs=[VMEM] * ZS if last else VMEM,
        scratch_shapes=[pltpu.VMEM(whole, jnp.float32)] if last else [],
        input_output_aliases={} if first or last else {len(operands) - 1: 0},
        compiler_params=pltpu.CompilerParams(vmem_limit_bytes=16 << 20),
        cost_estimate=pl.CostEstimate(
            flops=sum(len(p) for p in sources) * 400_000_000,
            transcendentals=0,
            bytes_accessed=6_000_000,
        ),
    )(*operands)


NOTE = 8
BASE = 4
ZS = 4
DIRECT = (1, 2)
FLOWS = ((1, 1), (0, 3), (1, 3), (0, 1), (0, 2), (1, 0))
EARLY = 3
AHEAD = 3


def after(x, y):
    return lax.optimization_barrier((x, y))


def on_device(pulses, footprint, offsets, azimuth, range_interp):
    held, _, width, _ = range_interp.shape
    owners = lax.axis_size("tile")
    pin = lambda x: pltpu.with_memory_space_constraint(x, pltpu.HBM)
    block = pin(pulses.reshape(-1, pulses.shape[-1]))
    footprint = pin(footprint.reshape(-1))
    slots = footprint.shape[0] // owners
    azimuth = azimuth[:, :, 0]
    send = lambda x, dy, dx, dc: lax.ppermute(x, "tile", pairs(owners, dy, dx, dc))
    cut = functools.partial(
        cut_windows,
        footprint=footprint,
        offsets=pin(offsets),
        block=block,
        held=held,
        slots=slots,
        width=width,
    )
    lead = [(0, (*DIRECT, 0)), (1, (*DIRECT, 1))]
    flows, made = [DIRECT], []
    for at, group in enumerate((FLOWS[:EARLY], FLOWS[EARLY:])):
        to = [(*f, 1) for f in group] + ([(0, 0, 1)] if at == 0 else [])
        extra = [lead] if at == 0 else []
        *first, other = cut([*extra, list(enumerate(to))], [2] * len(extra) + [len(to)], [])
        made += first
        other = send(other, 0, 0, 1)
        other, cut.keywords["footprint"] = after(other, cut.keywords["footprint"])
        to = [(*f, 0) for f in group] + ([(0, 0, 0)] if at == 0 else [])
        filled = cut(
            [[(0, t)] for t in to],
            [2] * len(to),
            [(n, n, 1) for n in range(len(to))],
            swapped=other,
        )
        flows += group
        made += filled[: len(group)]
        if at == 0:
            here = filled[-1]
    work = [([here], [[(0, 0, 0), (0, 0, 1)]])]
    sub, done = None, 0
    for f, (flow, w) in enumerate(zip(flows, made)):
        while done <= f - AHEAD:
            sub = add(work[done][1], slots, work[done][0], azimuth, range_interp, sub, False)
            done += 1
            w, sub = after(w, sub)
        w = send(w, *flow, 0)
        if f == 0:
            work.append(([w[:1], send(w[1:], 0, 0, 1)], [[(*flow, 0)], [(*flow, 1)]]))
        else:
            work.append(([w], [[(*flow, 0), (*flow, 1)]]))
    for windows, chips in work[done:-1]:
        sub = add(chips, slots, windows, azimuth, range_interp, sub, False)
    own, *away = add(work[-1][1], slots, work[-1][0], azimuth, range_interp, sub, True)

    subaps = lax.axis_size("subap")
    near = lambda x, dy, dz: lax.ppermute(
        x,
        "subap",
        [(i, (i // ZS ^ dy) * ZS + (i + dz) % ZS) for i in range(subaps)],
    )
    order = sorted(range(1, ZS), key=lambda dz: -min(dz, ZS - dz))
    for part in [near(away[dz - 1], 0, dz) for dz in order]:
        own = own + part.astype(jnp.float32)
    raw = own + near(own.astype(jnp.bfloat16), 1, 0).astype(jnp.float32)
    total = jnp.sum(raw * raw, axis=(1, 2, 3))
    total = total + sum(near(total, 0, dz) for dz in order)
    power = total / (raw[0].size * ZS)
    rows = raw.shape[2] // 2
    raw = lax.dynamic_slice_in_dim(raw, lax.axis_index("subap") // ZS * rows, rows, 2)
    return raw / jnp.sqrt(power + 1e-06)[:, None, None, None]


def solution(mesh):
    in_specs = (
        P("tile", "subap", None, None, None),
        P("tile", "subap", None),
        P(),
        P("tile", None, "subap", None, None, None),
        P("tile", None, None, None),
    )
    out_specs = P("tile", None, "subap", None)
    return jax.shard_map(
        on_device, mesh=mesh, in_specs=in_specs, out_specs=out_specs, check_vma=False
    )
```

```python
import functools

import jax
import jax.numpy as jnp
from jax import lax
from jax.experimental import pallas as pl
from jax.experimental.pallas import tpu as pltpu
from jax.sharding import PartitionSpec as P

LANES = 128
XS, CORES = 4, 2
ANY = pl.BlockSpec(memory_space=pl.ANY)
HBM = pl.BlockSpec(memory_space=pltpu.HBM)
VMEM = pl.BlockSpec(memory_space=pltpu.VMEM)


def place(index):
    return index // (XS * CORES), index // CORES % XS, index % CORES


def toward(index, dy, dx, dc):
    y, x, c = place(index)
    return ((y ^ dy) * XS + (x + dx) % XS) * CORES + (c ^ dc)


def pairs(count, dy, dx, dc):
    return [(i, toward(i, dy, dx, dc)) for i in range(count)]


def cut_kernel(pieces, fills, held, footprint_hbm, offsets_hbm, block, *refs):
    swapped, refs = (refs[0], refs[1:]) if fills else (None, refs)
    outs, refs = refs[: len(pieces)], refs[len(pieces) :]
    footprint, offsets, wide, cut, note, scalar_sem, in_sem, out_sem, note_sem, fill_sem = refs
    scalars = [
        pltpu.make_async_copy(footprint_hbm, footprint, scalar_sem.at[0]),
        pltpu.make_async_copy(offsets_hbm, offsets, scalar_sem.at[1]),
    ]
    for copy in scalars:
        copy.start()
    filling = []
    for n, (source, piece, at) in enumerate(fills):
        filling.append(
            pltpu.make_async_copy(swapped.at[source], outs[piece].at[at], fill_sem.at[n])
        )
        filling[-1].start()
    me = lax.axis_index("tile")
    rows, span = wide.shape[1:]
    width = cut.shape[2]
    slots = outs[0].shape[1] // rows
    lane = lax.broadcasted_iota(jnp.int32, note.shape[1:], 1)
    for copy in scalars:
        copy.wait()
    steps, notes = [], []
    for out, parts in zip(outs, pieces):
        for at, to in parts:
            owner = toward(me, *to)
            ids = jnp.zeros(lane.shape, jnp.int32)
            for slot in range(slots):
                tile = footprint[owner * slots + slot]
                start = offsets[tile]
                base = jnp.minimum(start // LANES * LANES, block.shape[1] - span)
                i = len(steps)
                src = block.at[:, pl.ds(pl.multiple_of(base, LANES), span)]
                get = pltpu.make_async_copy(src, wide.at[i], in_sem.at[i])
                dst = out.at[at, slot * rows : (slot + 1) * rows]
                put = pltpu.make_async_copy(cut.at[i], dst, out_sem.at[i])
                get.start()
                steps.append((get, put, start - base))
                ids = jnp.where(lane // LANES == slot, tile - owner * held, ids)
            j = len(notes)
            note[j] = ids.astype(note.dtype)
            told = pltpu.make_async_copy(note.at[j], out.at[at, slots * rows :], note_sem.at[j])
            told.start()
            notes.append(told)
    for i, (get, put, shift) in enumerate(steps):
        get.wait()
        turn = lax.rem(LANES - shift, LANES)
        inside = lax.broadcasted_iota(jnp.int32, (rows, LANES), 1) < LANES - shift
        turned = [
            pltpu.roll(wide[i, :, n * LANES : (n + 1) * LANES].astype(jnp.float32), turn, 1)
            for n in range(span // LANES)
        ]
        for n in range(width // LANES):
            cut[i, :, n * LANES : (n + 1) * LANES] = jnp.where(
                inside, turned[n], turned[n + 1]
            ).astype(cut.dtype)
        put.start()
    for _, put, _ in steps:
        put.wait()
    for copy in notes + filling:
        copy.wait()


def cut_windows(pieces, sizes, fills, footprint, offsets, block, held, slots, width, swapped=None):
    rows = block.shape[0]
    span = width + LANES
    whole = sum(len(parts) for parts in pieces)
    count = slots * whole
    operands = (footprint, offsets, block) + (() if swapped is None else (swapped,))
    return pl.pallas_call(
        functools.partial(cut_kernel, pieces, fills, held),
        out_shape=[
            jax.ShapeDtypeStruct((size, slots * rows + NOTE, width), block.dtype)
            for size in sizes
        ],
        in_specs=[HBM] * len(operands),
        out_specs=[ANY] * len(pieces),
        scratch_shapes=[
            pltpu.SMEM(footprint.shape, footprint.dtype),
            pltpu.SMEM(offsets.shape, offsets.dtype),
            pltpu.VMEM((count, rows, span), block.dtype),
            pltpu.VMEM((count, rows, width), block.dtype),
            pltpu.VMEM((whole, NOTE, width), block.dtype),
            pltpu.SemaphoreType.DMA((2,)),
            pltpu.SemaphoreType.DMA((count,)),
            pltpu.SemaphoreType.DMA((count,)),
            pltpu.SemaphoreType.DMA((whole,)),
            pltpu.SemaphoreType.DMA((max(len(fills), 1),)),
        ],
        compiler_params=pltpu.CompilerParams(vmem_limit_bytes=16 << 20),
        cost_estimate=pl.CostEstimate(
            flops=0, transcendentals=0, bytes_accessed=1000
        ),
    )(*operands)


def add_kernel(sources, slots, first, last, *refs):
    count = len(sources)
    windows, refs = refs[:count], refs[count:]
    azimuth, table, refs = refs[0], refs[1], refs[2:]
    if first:
        (sub,) = refs
        sub[...] = jnp.zeros_like(sub)
    else:
        before, refs = refs[0], refs[1:]
        outs, sub = (refs[:-1], refs[-1]) if last else ((), refs[0])
        sub[...] = before[...]
    me = lax.axis_index("tile")
    both = (windows[0].shape[1] - NOTE) // slots
    half = both // 2
    work, packed = [], None
    for window, parts in zip(windows, sources):
        for at, (dy, dx, dc) in enumerate(parts):
            note = window[at, slots * both :, :].astype(jnp.float32)
            for slot in range(slots):
                ids = note[:, slot * LANES : (slot + 1) * LANES] * float(BASE ** len(work))
                packed = ids if packed is None else packed + ids
                x = (window, at, slice(slot * both, (slot + 1) * both))
                work.append((x, toward(me, dy, XS - dx, dc)))
    packed = jnp.max(packed).astype(jnp.int32)
    def in_range(n):
        (window, at, span), source = work[n]
        tile = (packed >> (n * (BASE.bit_length() - 1))) & (BASE - 1)
        x = window[at, span]
        pr = jnp.dot(x, table[tile, 0], preferred_element_type=jnp.float32)
        pi = jnp.dot(x, table[tile, 1], preferred_element_type=jnp.float32)
        rr = (pr[:half] - pi[half:]).astype(x.dtype)
        ri = (pi[:half] + pr[half:]).astype(x.dtype)
        return tile, source, rr, ri

    def in_azimuth(tile, source, rr, ri):
        left = jnp.concatenate([azimuth[tile, source, 0], azimuth[tile, source, 1]], 1)
        right = jnp.concatenate(
            [jnp.concatenate([rr, ri], 1), jnp.concatenate([-ri, rr], 1)], 0
        )
        both = jnp.dot(left, right, preferred_element_type=jnp.float32)
        sub[tile, 0] += both[:, : rr.shape[1]]
        sub[tile, 1] += both[:, rr.shape[1] :]

    for ranged in [in_range(n) for n in range(len(work))]:
        in_azimuth(*ranged)
    if last:
        z = lax.axis_index("subap") % ZS
        halves = sub.shape[2] // outs[0].shape[2] // ZS * 2
        rows = outs[0].shape[2] // halves
        for dz, out in enumerate(outs):
            for y in range(halves):
                at = pl.multiple_of(((z + dz) % ZS + y * ZS) * rows, rows)
                out[:, :, y * rows : (y + 1) * rows] = sub[:, :, pl.ds(at, rows)].astype(out.dtype)


def add(sources, slots, windows, azimuth, table, before, last):
    tiles, _, parts, height, _ = azimuth.shape
    whole = (tiles, parts, height, table.shape[3])
    first = before is None
    shape = jax.ShapeDtypeStruct(whole, jnp.float32)
    if last:
        cut = (tiles, parts, height // ZS, table.shape[3])
        shape = [
            jax.ShapeDtypeStruct(cut, jnp.bfloat16 if dz else jnp.float32) for dz in range(ZS)
        ]
    operands = (*windows, azimuth, table) + (() if first else (before,))
    return pl.pallas_call(
        functools.partial(add_kernel, sources, slots, first, last),
        out_shape=shape,
        in_specs=[VMEM] * len(operands),
        out_specs=[VMEM] * ZS if last else VMEM,
        scratch_shapes=[pltpu.VMEM(whole, jnp.float32)] if last else [],
        input_output_aliases={} if first or last else {len(operands) - 1: 0},
        compiler_params=pltpu.CompilerParams(vmem_limit_bytes=16 << 20),
        cost_estimate=pl.CostEstimate(
            flops=sum(len(p) for p in sources) * 400_000_000,
            transcendentals=0,
            bytes_accessed=6_000_000,
        ),
    )(*operands)


NOTE = 8
BASE = 4
ZS = 4
DIRECT = (1, 2)
FLOWS = ((1, 1), (0, 3), (1, 3), (0, 1), (1, 0), (0, 2))
EARLY = 3
AHEAD = 3


def after(x, y):
    return lax.optimization_barrier((x, y))


def on_device(pulses, footprint, offsets, azimuth, range_interp):
    held, _, width, _ = range_interp.shape
    owners = lax.axis_size("tile")
    pin = lambda x: pltpu.with_memory_space_constraint(x, pltpu.HBM)
    block = pin(pulses.reshape(-1, pulses.shape[-1]))
    footprint = pin(footprint.reshape(-1))
    slots = footprint.shape[0] // owners
    azimuth = azimuth[:, :, 0]
    send = lambda x, dy, dx, dc: lax.ppermute(x, "tile", pairs(owners, dy, dx, dc))
    cut = functools.partial(
        cut_windows,
        footprint=footprint,
        offsets=pin(offsets),
        block=block,
        held=held,
        slots=slots,
        width=width,
    )
    lead = [(0, (*DIRECT, 0)), (1, (*DIRECT, 1))]
    flows, made = [DIRECT], []
    for at, group in enumerate((FLOWS[:EARLY], FLOWS[EARLY:])):
        to = [(*f, 1) for f in group] + ([(0, 0, 1)] if at == 0 else [])
        extra = [lead] if at == 0 else []
        *first, other = cut([*extra, list(enumerate(to))], [2] * len(extra) + [len(to)], [])
        made += first
        other = send(other, 0, 0, 1)
        other, cut.keywords["footprint"] = after(other, cut.keywords["footprint"])
        to = [(*f, 0) for f in group] + ([(0, 0, 0)] if at == 0 else [])
        filled = cut(
            [[(0, t)] for t in to],
            [2] * len(to),
            [(n, n, 1) for n in range(len(to))],
            swapped=other,
        )
        flows += group
        made += filled[: len(group)]
        if at == 0:
            here = filled[-1]
    work = [([here], [[(0, 0, 0), (0, 0, 1)]])]
    sub, done = None, 0
    for f, (flow, w) in enumerate(zip(flows, made)):
        while done <= f - AHEAD:
            sub = add(work[done][1], slots, work[done][0], azimuth, range_interp, sub, False)
            done += 1
            w, sub = after(w, sub)
        w = send(w, *flow, 0)
        if f == 0:
            work.append(([w[:1], send(w[1:], 0, 0, 1)], [[(*flow, 0)], [(*flow, 1)]]))
        else:
            work.append(([w], [[(*flow, 0), (*flow, 1)]]))
    for windows, chips in work[done:-1]:
        sub = add(chips, slots, windows, azimuth, range_interp, sub, False)
    own, *away = add(work[-1][1], slots, work[-1][0], azimuth, range_interp, sub, True)

    subaps = lax.axis_size("subap")
    near = lambda x, dy, dz: lax.ppermute(
        x,
        "subap",
        [(i, (i // ZS ^ dy) * ZS + (i + dz) % ZS) for i in range(subaps)],
    )
    order = sorted(range(1, ZS), key=lambda dz: -min(dz, ZS - dz))
    for part in [near(away[dz - 1], 0, dz) for dz in order]:
        own = own + part.astype(jnp.float32)
    raw = own + near(own.astype(jnp.bfloat16), 1, 0).astype(jnp.float32)
    total = jnp.sum(raw * raw, axis=(1, 2, 3))
    total = total + sum(near(total, 0, dz) for dz in order)
    power = total / (raw[0].size * ZS)
    rows = raw.shape[2] // 2
    raw = lax.dynamic_slice_in_dim(raw, lax.axis_index("subap") // ZS * rows, rows, 2)
    return raw / jnp.sqrt(power + 1e-06)[:, None, None, None]


def solution(mesh):
    in_specs = (
        P("tile", "subap", None, None, None),
        P("tile", "subap", None),
        P(),
        P("tile", None, "subap", None, None, None),
        P("tile", None, None, None),
    )
    out_specs = P("tile", None, "subap", None)
    return jax.shard_map(
        on_device, mesh=mesh, in_specs=in_specs, out_specs=out_specs, check_vma=False
    )
```
